32 devices in a mesh: seq: 8 (over z, y), chan: 4 (over x, core).
Axes of the slice: x: 2, y: 2, z: 4, core: 2. Of those that a mesh axis runs over, the one named last changes fastest.
Arguments:
- value: bfloat16 [1024, 4096], P('seq', 'chan'), may hold values from -6 to 6
- gate: bfloat16 [1024, 4096], P('seq', 'chan'), may hold values from -6 to 6
- long_filter: bfloat16 [4096, 1024], P('chan', 'seq'), may hold values from -0.5 to 0.5
- skip_gain: float32 [4096], P('chan'), may hold values from 0.5 to 2
- cotangent: bfloat16 [1024, 4096], P('seq', 'chan'), may hold values from -6 to 6
- owner_map: int32 [8], replicated, may hold values from 0 to 7, each once
Outputs:
- output: bfloat16 [1024, 4096], P('seq', 'chan')
- value_grad: bfloat16 [1024, 4096], P('seq', 'chan')
- gate_grad: bfloat16 [1024, 4096], P('seq', 'chan')
- gain_grad: float32 [4, 8, 128], P('chan', 'seq')
The draws below stay inside these ranges and needn't reach their ends.
Inputs may be any that keep to these rules, and one draw needn't show every extreme that they name: `owner_map`: a permutation: each index of seq once.
All inputs are finite; a program needn't handle non-finite values.
Results may differ from the reference program's by a relative error of at most 0.008.
Values may be sent and summed in bfloat16 or wider, within the bound.
A program may use at most 64 MiB of HBM per device.

```python
import math
import jax
import jax.numpy as jnp
from jax import lax

C = 4096
SEQ_LEN = 1024
BLOCK_ROWS = 128
N_SEQ = 8
N_CHAN = 4


def block_scale(key, shape, shards, smallest, top_value):
    loudness, own = 1.0, jax.random.fold_in(key, 6)
    for dim, blocks in shards:
        steps = jnp.exp(jax.random.uniform(jax.random.fold_in(own, dim), (blocks,), jnp.float32, smallest / len(shards), top_value / len(shards)))
        loudness = loudness * jnp.repeat(steps, shape[dim] // blocks).reshape([-1 if axis == dim else 1 for axis in range(len(shape))])
    return loudness


def centred(stream_key, shape, spread, reach, cuts=(), kind=jnp.bfloat16):
    entries = jax.random.normal(stream_key, shape, jnp.float32) * spread
    if len(cuts) > 0:
        entries = block_scale(stream_key, shape, cuts, -0.22, 0.18) * entries
    return jnp.clip(entries, min=-reach, max=reach).astype(kind)


def setup_inputs(seed: int = 0) -> dict:
    arg_keys = jax.random.split(jax.random.key(seed), 7)
    value = centred(arg_keys[0], (SEQ_LEN, C), 1.0, 6.0, ((0, 8), (1, 4)))
    gate = centred(arg_keys[1], (SEQ_LEN, C), 1.0, 6.0, ((0, 8), (1, 4)))
    long_filter = centred(arg_keys[2], (C, SEQ_LEN), (SEQ_LEN ** -0.5), 0.5, ((0, 4), (1, 8)))
    skip_gain = jnp.clip(0.5 + 1.5 * jax.random.uniform(arg_keys[3], (C,), jnp.float32) ** block_scale(arg_keys[3], (C,), ((0, 4),), -0.2, 0.2), 0.5, 2.0)
    cotangent = centred(arg_keys[4], (SEQ_LEN, C), 1.0, 6.0, ((0, 8), (1, 4)))
    owner_map = jax.random.permutation(arg_keys[5], N_SEQ).astype(jnp.int32)
    return dict(value=value, gate=gate, long_filter=long_filter, skip_gain=skip_gain, cotangent=cotangent, owner_map=owner_map)


def reference(value, gate, long_filter, skip_gain, cotangent, owner_map):
    length = value.shape[0]
    value_f = value.astype(jnp.float32)
    gate_f = gate.astype(jnp.float32)
    grad_conv = (cotangent.astype(jnp.float32) * gate_f).astype(jnp.bfloat16)
    padded = 2 * length
    filter_spec = jnp.fft.rfft(long_filter.astype(jnp.float32), n=padded, axis=1)
    value_spec = jnp.fft.rfft(value_f.T, n=padded, axis=1)
    conv = jnp.fft.irfft(value_spec * filter_spec, n=padded, axis=1)[:, :length].astype(jnp.bfloat16)
    grad_spec = jnp.fft.rfft(grad_conv.astype(jnp.float32).T, n=padded, axis=1)
    back_conv = jnp.fft.irfft(grad_spec * jnp.conj(filter_spec), n=padded, axis=1)[:, :length].astype(jnp.bfloat16)
    mixed = conv.T.astype(jnp.float32) + skip_gain * value_f
    output = (gate_f * mixed).astype(jnp.bfloat16)
    gate_grad = (cotangent.astype(jnp.float32) * mixed).astype(jnp.bfloat16)
    value_grad = (back_conv.T.astype(jnp.float32) + skip_gain * grad_conv.astype(jnp.float32)).astype(jnp.bfloat16)
    scale = 1.0 / math.sqrt(length)
    skip_grad = lax.optimization_barrier(jnp.sum(value_f * grad_conv.astype(jnp.float32), axis=0)) * scale
    blocked = skip_grad.reshape(N_CHAN, N_SEQ, BLOCK_ROWS)
    gain_grad = jnp.take(blocked, owner_map.astype(jnp.int32), axis=1)
    return (output, value_grad, gate_grad, gain_grad)
```

```python
import functools
import math

import jax
import jax.numpy as jnp
import numpy as np
from jax import lax
from jax.experimental import pallas as pl
from jax.experimental.pallas import tpu as pltpu
from jax.sharding import PartitionSpec as P

HIGHEST = lax.Precision.HIGHEST


def dft_table(size):
    index = jnp.arange(size, dtype=jnp.int32)
    phase = index[:, None] * index[None, :] % size
    angle = 2.0 * math.pi / size * phase.astype(jnp.float32)
    return (jnp.cos(angle), jnp.sin(angle))


def make_tables(outer, inner):
    cos_outer, sin_outer = dft_table(outer)
    cos_inner, sin_inner = dft_table(inner)
    total = outer * inner
    phase = (
        jnp.arange(outer, dtype=jnp.int32)[:, None]
        * jnp.arange(inner, dtype=jnp.int32)[None, :]
        % total
    )
    angle = 2.0 * math.pi / total * phase.astype(jnp.float32)
    return (cos_outer, sin_outer, cos_inner, sin_inner, jnp.cos(angle), jnp.sin(angle))


def forward_dft(signal, tables):
    cos_outer, sin_outer, cos_inner, sin_inner, turn_cos, turn_sin = tables
    blocks = signal.shape[0]
    real_part = jnp.einsum("kn,ncb->ckb", cos_outer[:, :blocks], signal, precision=HIGHEST)
    imag_part = -jnp.einsum("kn,ncb->ckb", sin_outer[:, :blocks], signal, precision=HIGHEST)
    twisted_real = real_part * turn_cos + imag_part * turn_sin
    twisted_imag = imag_part * turn_cos - real_part * turn_sin
    spec_real = jnp.einsum("ckn,nm->ckm", twisted_real, cos_inner, precision=HIGHEST) + jnp.einsum(
        "ckn,nm->ckm", twisted_imag, sin_inner, precision=HIGHEST
    )
    spec_imag = jnp.einsum("ckn,nm->ckm", twisted_imag, cos_inner, precision=HIGHEST) - jnp.einsum(
        "ckn,nm->ckm", twisted_real, sin_inner, precision=HIGHEST
    )
    return (spec_real, spec_imag)


def inverse_dft(spec_real, spec_imag, tables, blocks):
    cos_outer, sin_outer, cos_inner, sin_inner, turn_cos, turn_sin = tables
    total = cos_outer.shape[0] * cos_inner.shape[0]
    inner_real = jnp.einsum("ckm,mn->ckn", spec_real, cos_inner, precision=HIGHEST) - jnp.einsum(
        "ckm,mn->ckn", spec_imag, sin_inner, precision=HIGHEST
    )
    inner_imag = jnp.einsum("ckm,mn->ckn", spec_real, sin_inner, precision=HIGHEST) + jnp.einsum(
        "ckm,mn->ckn", spec_imag, cos_inner, precision=HIGHEST
    )
    turned_real = inner_real * turn_cos - inner_imag * turn_sin
    turned_imag = inner_real * turn_sin + inner_imag * turn_cos
    result = jnp.einsum(
        "nk,ckb->ncb", cos_outer[:blocks, :], turned_real, precision=HIGHEST
    ) - jnp.einsum("nk,ckb->ncb", sin_outer[:blocks, :], turned_imag, precision=HIGHEST)
    return result / total


def causal_conv(sent_value, filter_spec, tables):
    value_real, value_imag = forward_dft(sent_value.astype(jnp.float32), tables)
    filter_real, filter_imag = filter_spec
    product_real = value_real * filter_real - value_imag * filter_imag
    product_imag = value_real * filter_imag + value_imag * filter_real
    return inverse_dft(product_real, product_imag, tables, sent_value.shape[0]).astype(jnp.bfloat16)


def transposed_conv(sent_grad, filter_spec, tables):
    grad_real, grad_imag = forward_dft(sent_grad.astype(jnp.float32), tables)
    filter_real, filter_imag = filter_spec
    product_real = grad_real * filter_real + grad_imag * filter_imag
    product_imag = grad_imag * filter_real - grad_real * filter_imag
    return inverse_dft(product_real, product_imag, tables, sent_grad.shape[0]).astype(jnp.bfloat16)


def split_body(value, gate, long_filter, skip_gain, cotangent, owner_map):
    blocks = lax.axis_size("seq")
    tok_rows = value.shape[0]
    group = value.shape[1]
    per_device = group // blocks
    value_rows = value.astype(jnp.float32)
    gate_rows = gate.astype(jnp.float32)
    grad_rows = (cotangent.astype(jnp.float32) * gate_rows).astype(jnp.bfloat16)
    value_major = value.T
    grad_major = grad_rows.T
    tables = make_tables(2 * blocks, tok_rows)
    value_split = value_major.reshape(blocks, per_device, tok_rows)
    filter_split = long_filter.reshape(blocks, per_device, tok_rows)
    grad_split = grad_major.reshape(blocks, per_device, tok_rows)
    sent_value, sent_filter = (
        lax.all_to_all(value_split, "seq", split_axis=0, concat_axis=0, tiled=True),
        lax.all_to_all(filter_split, "seq", split_axis=0, concat_axis=0, tiled=True),
    )
    filter_spec = forward_dft(sent_filter.astype(jnp.float32), tables)
    conv_back = lax.all_to_all(
        causal_conv(sent_value, filter_spec, tables), "seq", split_axis=0, concat_axis=0, tiled=True
    )
    sent_grad = lax.all_to_all(grad_split, "seq", split_axis=0, concat_axis=0, tiled=True)
    grad_back = lax.all_to_all(
        transposed_conv(sent_grad, filter_spec, tables),
        "seq",
        split_axis=0,
        concat_axis=0,
        tiled=True,
    )
    conv_rows = conv_back.reshape(group, tok_rows).T.astype(jnp.float32)
    mixed = conv_rows + skip_gain * value_rows
    output = (gate_rows * mixed).astype(jnp.bfloat16)
    gate_grad = (cotangent.astype(jnp.float32) * mixed).astype(jnp.bfloat16)
    back_rows = grad_back.reshape(group, tok_rows).T.astype(jnp.float32)
    grad_float = grad_rows.astype(jnp.float32)
    value_grad = (back_rows + skip_gain * grad_float).astype(jnp.bfloat16)
    scale = 1.0 / math.sqrt(tok_rows * blocks)
    local_sums = (
        jnp.sum(sent_value.astype(jnp.float32) * sent_grad.astype(jnp.float32), axis=(0, 2)) * scale
    )
    gathered = lax.all_gather(local_sums.reshape(1, per_device), "seq", axis=0, tiled=True)
    mine = owner_map[lax.axis_index("seq")]
    summed = lax.dynamic_slice_in_dim(gathered, mine, 1, 0)
    gain_grad = summed.reshape(1, 1, per_device)
    return (output, value_grad, gate_grad, gain_grad)


LANES = 128
FILTER, VALUE, GRAD, CONV, BACK, SUMS = range(6)
MESH = pl.DeviceIdType.MESH


def base_tables(length):
    unit = 2.0 * math.pi / (16 * length)
    row = 4 * np.arange(length, dtype=np.int64)[:, None] + 1
    lane = 4 * np.arange(LANES, dtype=np.int64)[None, :] + 1
    angle = unit * (row * lane % (16 * length))
    block = 4 * LANES * np.arange(length // LANES, dtype=np.int64)[None, :]
    step = unit * (row * block % (16 * length))
    quarter = unit * row
    turn = np.concatenate([np.cos(step), np.sin(step), np.cos(quarter), np.sin(quarter)], axis=1)
    turn = np.pad(turn, ((0, 0), (0, -turn.shape[1] % LANES)))
    return tuple(t.astype(np.float32) for t in (np.cos(angle), np.sin(angle), turn))


def split(wide):
    high = wide.astype(jnp.bfloat16)
    return high, (wide - high.astype(jnp.float32)).astype(jnp.bfloat16)


def fused_kernel(
    n,
    value,
    filt,
    gate,
    cot,
    skip,
    owner,
    base_cos,
    base_sin,
    turn,
    out,
    value_grad,
    gate_grad,
    gain,
    value_loc,
    gate_loc,
    cot_loc,
    grad_loc,
    cos_hi,
    cos_lo,
    sin_hi,
    sin_lo,
    seq_value,
    seq_filter,
    taps,
    seq_grad,
    spec_c,
    spec_d,
    spec_a,
    spec_b,
    prod_cos,
    prod_sin,
    conv_out,
    back_out,
    conv_in,
    back_in,
    sums_out,
    sums_in,
    send_sem,
    recv_sem,
    local_sem,
):
    me = lax.axis_index("seq")
    rows, group = value.shape
    chans = group // n
    length = rows * n
    half = length // 2
    offsets = sorted(range(1, n), key=lambda i: abs(2 * i - n))
    blocks = length // LANES

    def peer_of(offset):
        return lax.rem(me + offset, n)

    def cols(index):
        return pl.ds(pl.multiple_of(index * chans, chans), chans)

    def seq_rows(index):
        return pl.ds(pl.multiple_of(index * rows, rows), rows)

    def transfer(kind, source, target, peer, sender):
        return pltpu.make_async_remote_copy(
            src_ref=source,
            dst_ref=target,
            send_sem=send_sem.at[kind, peer],
            recv_sem=recv_sem.at[kind, sender],
            device_id={"seq": peer},
            device_id_type=MESH,
        )

    def copy_of(kind, peer, sender):
        if kind == FILTER:
            pair = filt.at[cols(peer), :], seq_filter.at[sender]
        elif kind == VALUE:
            pair = value.at[:, cols(peer)], seq_value.at[seq_rows(sender), :]
        elif kind == GRAD:
            pair = grad_loc.at[:, cols(peer)], seq_grad.at[seq_rows(sender), :]
        elif kind == CONV:
            pair = conv_out.at[seq_rows(peer), :], conv_in.at[sender]
        elif kind == BACK:
            pair = back_out.at[seq_rows(peer), :], back_in.at[sender]
        else:
            pair = sums_out, sums_in.at[sender]
        return transfer(kind, *pair, peer, sender)

    def send(kind, peer):
        copy_of(kind, peer, me).start()

    def receive(kind):
        for offset in reversed(offsets):
            peer = peer_of(offset)
            copy_of(kind, peer, peer).wait_recv()

    barrier = pltpu.get_barrier_semaphore()
    for offset in offsets:
        pl.semaphore_signal(barrier, inc=1, device_id={"seq": peer_of(offset)}, device_id_type=MESH)
    local = [
        pltpu.make_async_copy(gate, gate_loc, local_sem.at[0]),
        pltpu.make_async_copy(cot, cot_loc, local_sem.at[1]),
        pltpu.make_async_copy(value, value_loc, local_sem.at[2]),
        pltpu.make_async_copy(filt.at[cols(me), :], seq_filter.at[me], local_sem.at[3]),
        pltpu.make_async_copy(value.at[:, cols(me)], seq_value.at[seq_rows(me), :], local_sem.at[4]),
    ]
    for copy in local:
        copy.start()
    pl.semaphore_wait(barrier, n - 1)
    for kind in (FILTER, VALUE):
        for offset in offsets:
            send(kind, peer_of(offset))

    local[0].wait()
    local[1].wait()
    grad_loc[...] = (cot_loc[...].astype(jnp.float32) * gate_loc[...].astype(jnp.float32)).astype(
        jnp.bfloat16
    )
    seq_grad[seq_rows(me), :] = grad_loc[:, cols(me)]
    for offset in offsets:
        send(GRAD, peer_of(offset))

    @pl.loop(0, length // LANES)
    def _(step):
        at = pl.ds(pl.multiple_of(step * LANES, LANES), LANES)
        lane_cos, lane_sin = base_cos[at, :], base_sin[at, :]
        for block in range(blocks):
            block_cos = turn[at, block : block + 1]
            block_sin = turn[at, blocks + block : blocks + block + 1]
            to = pl.ds(block * LANES, LANES)
            cos_hi[at, to], cos_lo[at, to] = split(lane_cos * block_cos - lane_sin * block_sin)
            sin_hi[at, to], sin_lo[at, to] = split(lane_sin * block_cos + lane_cos * block_sin)

    def forward(signal, real, imag):
        @pl.loop(0, 2)
        def _(step):
            at = pl.ds(pl.multiple_of(step * half, half), half)
            for high, low, spec in ((cos_hi, cos_lo, real), (sin_hi, sin_lo, imag)):
                spec[at, :] = jnp.dot(
                    high[at, :], signal[...], preferred_element_type=jnp.float32
                ) + jnp.dot(low[at, :], signal[...], preferred_element_type=jnp.float32)

    def put_product(on_cos, on_sin):
        for wide, store in ((on_cos, prod_cos), (on_sin, prod_sin)):
            high, low = split(wide)
            store[:, :chans] = high
            store[:, chans:] = low

    def inverse(result, kind):
        mine = me // (n // 2)

        @pl.loop(0, 2)
        def _(step):
            part = lax.rem(mine + 1 + step, 2)
            at = pl.ds(pl.multiple_of(part * half, half), half)
            both = jnp.dot(
                cos_hi[at, :], prod_cos[...], preferred_element_type=jnp.float32
            ) + jnp.dot(sin_hi[at, :], prod_sin[...], preferred_element_type=jnp.float32)
            low = jnp.dot(
                cos_lo[at, :], prod_cos[:, :chans], preferred_element_type=jnp.float32
            ) + jnp.dot(sin_lo[at, :], prod_sin[:, :chans], preferred_element_type=jnp.float32)
            result[at, :] = (both[:, :chans] + (both[:, chans:] + low)).astype(jnp.bfloat16)
            for index in range(n // 2):
                to = part * (n // 2) + lax.rem(me + index, n // 2)

                @pl.when(to != me)
                def _():
                    send(kind, to)

    local[3].wait()
    receive(FILTER)
    for index in range(n):
        taps[index * rows : (index + 1) * rows, :] = (
            seq_filter[index].astype(jnp.float32).T.astype(jnp.bfloat16)
        )
    forward(taps, spec_a, spec_b)
    quarter_cos = turn[:, 2 * blocks : 2 * blocks + 1] * (1.0 / length)
    quarter_sin = turn[:, 2 * blocks + 1 : 2 * blocks + 2] * (1.0 / length)
    spec_c[...] = spec_a[...] * quarter_cos + spec_b[...] * quarter_sin
    spec_d[...] = spec_b[...] * quarter_cos - spec_a[...] * quarter_sin

    local[4].wait()
    receive(VALUE)
    forward(seq_value, spec_a, spec_b)
    put_product(
        spec_a[...] * spec_c[...] - spec_b[...] * spec_d[...],
        spec_a[...] * spec_d[...] + spec_b[...] * spec_c[...],
    )
    inverse(conv_out, CONV)

    receive(GRAD)
    forward(seq_grad, spec_a, spec_b)
    put_product(
        spec_a[...] * spec_c[...] + spec_b[...] * spec_d[...],
        spec_b[...] * spec_c[...] - spec_a[...] * spec_d[...],
    )
    inverse(back_out, BACK)
    sums = jnp.sum(
        seq_value[...].astype(jnp.float32) * seq_grad[...].astype(jnp.float32), axis=0, keepdims=True
    ) * (1.0 / math.sqrt(length))
    sums_out[...] = jnp.broadcast_to(sums, sums_out.shape)
    sums_in[me] = jnp.broadcast_to(sums, sums_out.shape)
    for offset in offsets:
        send(SUMS, peer_of(offset))

    local[2].wait()

    def finish_conv(index, conv):
        at = cols(index)
        mixed = conv.astype(jnp.float32) + skip[:, at] * value_loc[:, at].astype(jnp.float32)
        out[:, at] = (gate_loc[:, at].astype(jnp.float32) * mixed).astype(jnp.bfloat16)
        gate_grad[:, at] = (cot_loc[:, at].astype(jnp.float32) * mixed).astype(jnp.bfloat16)

    def finish_back(index, back):
        at = cols(index)
        value_grad[:, at] = (
            back.astype(jnp.float32) + skip[:, at] * grad_loc[:, at].astype(jnp.float32)
        ).astype(jnp.bfloat16)

    finish_conv(me, conv_out[seq_rows(me), :])
    finish_back(me, back_out[seq_rows(me), :])
    for kind, finish, landed in ((CONV, finish_conv, conv_in), (BACK, finish_back, back_in)):
        for offset in reversed(offsets):
            peer = peer_of(offset)
            copy_of(kind, peer, peer).wait_recv()
            finish(peer, landed[peer])
    receive(SUMS)
    gain[...] = sums_in[owner[me]][:1, :]
    for kind in range(6):
        for offset in offsets:
            peer = peer_of(offset)
            copy_of(kind, peer, me).wait_send()


def fused_body(value, gate, long_filter, skip_gain, cotangent, owner_map):
    n = lax.axis_size("seq")
    rows, group = value.shape
    chans = group // n
    length = rows * n
    base_cos, base_sin, turn = base_tables(length)
    anywhere = pl.BlockSpec(memory_space=pl.ANY)
    vmem = pl.BlockSpec(memory_space=pltpu.VMEM)
    bf16, f32 = jnp.bfloat16, jnp.float32
    table = pltpu.VMEM((length, length), bf16)
    spec = pltpu.VMEM((length, chans), f32)
    tokens = pltpu.VMEM((rows, group), bf16)
    sequence = pltpu.VMEM((length, chans), bf16)
    landing = pltpu.VMEM((n, rows, chans), bf16)
    output, value_grad, gate_grad, gain = pl.pallas_call(
        functools.partial(fused_kernel, n),
        out_shape=(
            jax.ShapeDtypeStruct((rows, group), bf16),
            jax.ShapeDtypeStruct((rows, group), bf16),
            jax.ShapeDtypeStruct((rows, group), bf16),
            jax.ShapeDtypeStruct((1, chans), f32),
        ),
        in_specs=[
            anywhere,
            anywhere,
            anywhere,
            anywhere,
            vmem,
            pl.BlockSpec(memory_space=pltpu.SMEM),
            vmem,
            vmem,
            vmem,
        ],
        out_specs=(vmem, vmem, vmem, vmem),
        scratch_shapes=[
            tokens,
            tokens,
            tokens,
            tokens,
            table,
            table,
            table,
            table,
            sequence,
            pltpu.VMEM((n, chans, rows), bf16),
            sequence,
            sequence,
            spec,
            spec,
            spec,
            spec,
            pltpu.VMEM((length, 2 * chans), bf16),
            pltpu.VMEM((length, 2 * chans), bf16),
            sequence,
            sequence,
            landing,
            landing,
            pltpu.VMEM((8, chans), f32),
            pltpu.VMEM((n, 8, chans), f32),
            pltpu.SemaphoreType.DMA((6, n)),
            pltpu.SemaphoreType.DMA((6, n)),
            pltpu.SemaphoreType.DMA((5,)),
        ],
        compiler_params=pltpu.CompilerParams(collective_id=0, has_side_effects=True),
    )(
        value,
        long_filter,
        gate,
        cotangent,
        skip_gain.reshape(1, group),
        owner_map,
        base_cos,
        base_sin,
        turn,
    )
    return (output, value_grad, gate_grad, gain.reshape(1, 1, chans))


def body(value, gate, long_filter, skip_gain, cotangent, owner_map):
    n = lax.axis_size("seq")
    rows, group = value.shape
    aligned = rows % LANES == 0 and group % (n * LANES) == 0 and n % 2 == 0
    tables_fit = 8 * (rows * n) ** 2 <= 16 * 2**20
    chosen = fused_body if aligned and tables_fit else split_body
    return chosen(value, gate, long_filter, skip_gain, cotangent, owner_map)


def solution(mesh):
    in_specs = (
        P("seq", "chan"),
        P("seq", "chan"),
        P("chan", "seq"),
        P("chan"),
        P("seq", "chan"),
        P(),
    )
    out_specs = (P("seq", "chan"), P("seq", "chan"), P("seq", "chan"), P("chan", "seq", None))
    return jax.shard_map(body, mesh=mesh, in_specs=in_specs, out_specs=out_specs, check_vma=False)
```

```python
import functools
import math

import jax
import jax.numpy as jnp
import numpy as np
from jax import lax
from jax.experimental import pallas as pl
from jax.experimental.pallas import tpu as pltpu
from jax.sharding import PartitionSpec as P

HIGHEST = lax.Precision.HIGHEST


def dft_table(size):
    index = jnp.arange(size, dtype=jnp.int32)
    phase = index[:, None] * index[None, :] % size
    angle = 2.0 * math.pi / size * phase.astype(jnp.float32)
    return (jnp.cos(angle), jnp.sin(angle))


def make_tables(outer, inner):
    cos_outer, sin_outer = dft_table(outer)
    cos_inner, sin_inner = dft_table(inner)
    total = outer * inner
    phase = (
        jnp.arange(outer, dtype=jnp.int32)[:, None]
        * jnp.arange(inner, dtype=jnp.int32)[None, :]
        % total
    )
    angle = 2.0 * math.pi / total * phase.astype(jnp.float32)
    return (cos_outer, sin_outer, cos_inner, sin_inner, jnp.cos(angle), jnp.sin(angle))


def forward_dft(signal, tables):
    cos_outer, sin_outer, cos_inner, sin_inner, turn_cos, turn_sin = tables
    blocks = signal.shape[0]
    real_part = jnp.einsum("kn,ncb->ckb", cos_outer[:, :blocks], signal, precision=HIGHEST)
    imag_part = -jnp.einsum("kn,ncb->ckb", sin_outer[:, :blocks], signal, precision=HIGHEST)
    twisted_real = real_part * turn_cos + imag_part * turn_sin
    twisted_imag = imag_part * turn_cos - real_part * turn_sin
    spec_real = jnp.einsum("ckn,nm->ckm", twisted_real, cos_inner, precision=HIGHEST) + jnp.einsum(
        "ckn,nm->ckm", twisted_imag, sin_inner, precision=HIGHEST
    )
    spec_imag = jnp.einsum("ckn,nm->ckm", twisted_imag, cos_inner, precision=HIGHEST) - jnp.einsum(
        "ckn,nm->ckm", twisted_real, sin_inner, precision=HIGHEST
    )
    return (spec_real, spec_imag)


def inverse_dft(spec_real, spec_imag, tables, blocks):
    cos_outer, sin_outer, cos_inner, sin_inner, turn_cos, turn_sin = tables
    total = cos_outer.shape[0] * cos_inner.shape[0]
    inner_real = jnp.einsum("ckm,mn->ckn", spec_real, cos_inner, precision=HIGHEST) - jnp.einsum(
        "ckm,mn->ckn", spec_imag, sin_inner, precision=HIGHEST
    )
    inner_imag = jnp.einsum("ckm,mn->ckn", spec_real, sin_inner, precision=HIGHEST) + jnp.einsum(
        "ckm,mn->ckn", spec_imag, cos_inner, precision=HIGHEST
    )
    turned_real = inner_real * turn_cos - inner_imag * turn_sin
    turned_imag = inner_real * turn_sin + inner_imag * turn_cos
    result = jnp.einsum(
        "nk,ckb->ncb", cos_outer[:blocks, :], turned_real, precision=HIGHEST
    ) - jnp.einsum("nk,ckb->ncb", sin_outer[:blocks, :], turned_imag, precision=HIGHEST)
    return result / total


def causal_conv(sent_value, filter_spec, tables):
    value_real, value_imag = forward_dft(sent_value.astype(jnp.float32), tables)
    filter_real, filter_imag = filter_spec
    product_real = value_real * filter_real - value_imag * filter_imag
    product_imag = value_real * filter_imag + value_imag * filter_real
    return inverse_dft(product_real, product_imag, tables, sent_value.shape[0]).astype(jnp.bfloat16)


def transposed_conv(sent_grad, filter_spec, tables):
    grad_real, grad_imag = forward_dft(sent_grad.astype(jnp.float32), tables)
    filter_real, filter_imag = filter_spec
    product_real = grad_real * filter_real + grad_imag * filter_imag
    product_imag = grad_imag * filter_real - grad_real * filter_imag
    return inverse_dft(product_real, product_imag, tables, sent_grad.shape[0]).astype(jnp.bfloat16)


def split_body(value, gate, long_filter, skip_gain, cotangent, owner_map):
    blocks = lax.axis_size("seq")
    tok_rows = value.shape[0]
    group = value.shape[1]
    per_device = group // blocks
    value_rows = value.astype(jnp.float32)
    gate_rows = gate.astype(jnp.float32)
    grad_rows = (cotangent.astype(jnp.float32) * gate_rows).astype(jnp.bfloat16)
    value_major = value.T
    grad_major = grad_rows.T
    tables = make_tables(2 * blocks, tok_rows)
    value_split = value_major.reshape(blocks, per_device, tok_rows)
    filter_split = long_filter.reshape(blocks, per_device, tok_rows)
    grad_split = grad_major.reshape(blocks, per_device, tok_rows)
    sent_value, sent_filter = (
        lax.all_to_all(value_split, "seq", split_axis=0, concat_axis=0, tiled=True),
        lax.all_to_all(filter_split, "seq", split_axis=0, concat_axis=0, tiled=True),
    )
    filter_spec = forward_dft(sent_filter.astype(jnp.float32), tables)
    conv_back = lax.all_to_all(
        causal_conv(sent_value, filter_spec, tables), "seq", split_axis=0, concat_axis=0, tiled=True
    )
    sent_grad = lax.all_to_all(grad_split, "seq", split_axis=0, concat_axis=0, tiled=True)
    grad_back = lax.all_to_all(
        transposed_conv(sent_grad, filter_spec, tables),
        "seq",
        split_axis=0,
        concat_axis=0,
        tiled=True,
    )
    conv_rows = conv_back.reshape(group, tok_rows).T.astype(jnp.float32)
    mixed = conv_rows + skip_gain * value_rows
    output = (gate_rows * mixed).astype(jnp.bfloat16)
    gate_grad = (cotangent.astype(jnp.float32) * mixed).astype(jnp.bfloat16)
    back_rows = grad_back.reshape(group, tok_rows).T.astype(jnp.float32)
    grad_float = grad_rows.astype(jnp.float32)
    value_grad = (back_rows + skip_gain * grad_float).astype(jnp.bfloat16)
    scale = 1.0 / math.sqrt(tok_rows * blocks)
    local_sums = (
        jnp.sum(sent_value.astype(jnp.float32) * sent_grad.astype(jnp.float32), axis=(0, 2)) * scale
    )
    gathered = lax.all_gather(local_sums.reshape(1, per_device), "seq", axis=0, tiled=True)
    mine = owner_map[lax.axis_index("seq")]
    summed = lax.dynamic_slice_in_dim(gathered, mine, 1, 0)
    gain_grad = summed.reshape(1, 1, per_device)
    return (output, value_grad, gate_grad, gain_grad)


LANES = 128
FILTER, VALUE, GRAD, CONV, BACK, SUMS = range(6)
MESH = pl.DeviceIdType.MESH


def base_tables(length):
    unit = 2.0 * math.pi / (16 * length)
    row = 4 * np.arange(length, dtype=np.int64)[:, None] + 1
    lane = 4 * np.arange(LANES, dtype=np.int64)[None, :] + 1
    angle = unit * (row * lane % (16 * length))
    block = 4 * LANES * np.arange(length // LANES, dtype=np.int64)[None, :]
    step = unit * (row * block % (16 * length))
    quarter = unit * row
    turn = np.concatenate([np.cos(step), np.sin(step), np.cos(quarter), np.sin(quarter)], axis=1)
    turn = np.pad(turn, ((0, 0), (0, -turn.shape[1] % LANES)))
    return tuple(t.astype(np.float32) for t in (np.cos(angle), np.sin(angle), turn))


def split(wide):
    high = wide.astype(jnp.bfloat16)
    return high, (wide - high.astype(jnp.float32)).astype(jnp.bfloat16)


def fused_kernel(
    n,
    value,
    filt,
    gate,
    cot,
    skip,
    owner,
    base_cos_any,
    base_sin_any,
    turn_any,
    out,
    value_grad,
    gain,
    base_cos,
    base_sin,
    turn,
    value_loc,
    gate_loc,
    cot_loc,
    grad_loc,
    cos_hi,
    cos_lo,
    sin_hi,
    sin_lo,
    seq_value,
    seq_filter,
    taps,
    seq_grad,
    spec_c,
    spec_d,
    spec_a,
    spec_b,
    prod_cos,
    prod_sin,
    conv_out,
    back_out,
    conv_in,
    back_in,
    sums_out,
    sums_in,
    send_sem,
    recv_sem,
    local_sem,
):
    me = lax.axis_index("seq")
    rows, group = value.shape
    chans = group // n
    length = rows * n
    half = length // 2
    offsets = sorted(range(1, n), key=lambda i: abs(2 * i - n))
    blocks = length // LANES

    def peer_of(offset):
        return lax.rem(me + offset, n)

    def cols(index):
        return pl.ds(pl.multiple_of(index * chans, chans), chans)

    def seq_rows(index):
        return pl.ds(pl.multiple_of(index * rows, rows), rows)

    def transfer(kind, source, target, peer, sender):
        return pltpu.make_async_remote_copy(
            src_ref=source,
            dst_ref=target,
            send_sem=send_sem.at[kind, peer],
            recv_sem=recv_sem.at[kind, sender],
            device_id={"seq": peer},
            device_id_type=MESH,
        )

    def copy_of(kind, peer, sender):
        if kind == FILTER:
            pair = filt.at[cols(peer), :], seq_filter.at[sender]
        elif kind == VALUE:
            pair = value.at[:, cols(peer)], seq_value.at[seq_rows(sender), :]
        elif kind == GRAD:
            pair = grad_loc.at[:, cols(peer)], seq_grad.at[seq_rows(sender), :]
        elif kind == CONV:
            pair = conv_out.at[seq_rows(peer), :], conv_in.at[sender]
        elif kind == BACK:
            pair = back_out.at[seq_rows(peer), :], back_in.at[sender]
        else:
            pair = sums_out, sums_in.at[sender]
        return transfer(kind, *pair, peer, sender)

    def send(kind, peer):
        copy_of(kind, peer, me).start()

    def receive(kind):
        for offset in reversed(offsets):
            peer = peer_of(offset)
            copy_of(kind, peer, peer).wait_recv()

    barrier = pltpu.get_barrier_semaphore()
    for offset in offsets:
        pl.semaphore_signal(barrier, inc=1, device_id={"seq": peer_of(offset)}, device_id_type=MESH)
    local = [
        pltpu.make_async_copy(gate, gate_loc, local_sem.at[0]),
        pltpu.make_async_copy(cot, cot_loc, local_sem.at[1]),
        pltpu.make_async_copy(value, value_loc, local_sem.at[2]),
        pltpu.make_async_copy(filt.at[cols(me), :], seq_filter.at[me], local_sem.at[3]),
        pltpu.make_async_copy(value.at[:, cols(me)], seq_value.at[seq_rows(me), :], local_sem.at[4]),
        pltpu.make_async_copy(base_cos_any, base_cos, local_sem.at[5]),
        pltpu.make_async_copy(base_sin_any, base_sin, local_sem.at[6]),
        pltpu.make_async_copy(turn_any, turn, local_sem.at[7]),
    ]
    for copy in local:
        copy.start()
    pl.semaphore_wait(barrier, n - 1)
    for kind in (FILTER, VALUE):
        for offset in offsets:
            send(kind, peer_of(offset))

    local[0].wait()
    local[1].wait()
    grad_loc[...] = (cot_loc[...].astype(jnp.float32) * gate_loc[...].astype(jnp.float32)).astype(
        jnp.bfloat16
    )
    seq_grad[seq_rows(me), :] = grad_loc[:, cols(me)]
    for offset in offsets:
        send(GRAD, peer_of(offset))

    for copy in local[5:]:
        copy.wait()

    @pl.loop(0, length // LANES)
    def _(step):
        at = pl.ds(pl.multiple_of(step * LANES, LANES), LANES)
        lane_cos, lane_sin = base_cos[at, :], base_sin[at, :]
        for block in range(blocks):
            block_cos = turn[at, block : block + 1]
            block_sin = turn[at, blocks + block : blocks + block + 1]
            to = pl.ds(block * LANES, LANES)
            cos_hi[at, to], cos_lo[at, to] = split(lane_cos * block_cos - lane_sin * block_sin)
            sin_hi[at, to], sin_lo[at, to] = split(lane_sin * block_cos + lane_cos * block_sin)

    def forward(signal, real, imag):
        @pl.loop(0, 2)
        def _(step):
            at = pl.ds(pl.multiple_of(step * half, half), half)
            for high, low, spec in ((cos_hi, cos_lo, real), (sin_hi, sin_lo, imag)):
                spec[at, :] = jnp.dot(
                    high[at, :], signal[...], preferred_element_type=jnp.float32
                ) + jnp.dot(low[at, :], signal[...], preferred_element_type=jnp.float32)

    def put_product(on_cos, on_sin):
        for wide, store in ((on_cos, prod_cos), (on_sin, prod_sin)):
            high, low = split(wide)
            store[:, :chans] = high
            store[:, chans:] = low

    def inverse(result, kind):
        mine = me // (n // 2)

        @pl.loop(0, 2)
        def _(step):
            part = lax.rem(mine + 1 + step, 2)
            at = pl.ds(pl.multiple_of(part * half, half), half)
            both = jnp.dot(
                cos_hi[at, :], prod_cos[...], preferred_element_type=jnp.float32
            ) + jnp.dot(sin_hi[at, :], prod_sin[...], preferred_element_type=jnp.float32)
            low = jnp.dot(
                cos_lo[at, :], prod_cos[:, :chans], preferred_element_type=jnp.float32
            ) + jnp.dot(sin_lo[at, :], prod_sin[:, :chans], preferred_element_type=jnp.float32)
            result[at, :] = (both[:, :chans] + (both[:, chans:] + low)).astype(jnp.bfloat16)
            for index in range(n // 2):
                to = part * (n // 2) + lax.rem(me + index, n // 2)

                @pl.when(to != me)
                def _():
                    send(kind, to)

    local[3].wait()
    receive(FILTER)
    for index in range(n):
        taps[index * rows : (index + 1) * rows, :] = (
            seq_filter[index].astype(jnp.float32).T.astype(jnp.bfloat16)
        )
    forward(taps, spec_a, spec_b)
    quarter_cos = turn[:, 2 * blocks : 2 * blocks + 1] * (1.0 / length)
    quarter_sin = turn[:, 2 * blocks + 1 : 2 * blocks + 2] * (1.0 / length)
    spec_c[...] = spec_a[...] * quarter_cos + spec_b[...] * quarter_sin
    spec_d[...] = spec_b[...] * quarter_cos - spec_a[...] * quarter_sin

    local[4].wait()
    receive(VALUE)
    forward(seq_value, spec_a, spec_b)
    put_product(
        spec_a[...] * spec_c[...] - spec_b[...] * spec_d[...],
        spec_a[...] * spec_d[...] + spec_b[...] * spec_c[...],
    )
    inverse(conv_out, CONV)

    receive(GRAD)
    sums = jnp.sum(
        seq_value[...].astype(jnp.float32) * seq_grad[...].astype(jnp.float32), axis=0, keepdims=True
    ) * (1.0 / math.sqrt(length))
    sums_out[...] = jnp.broadcast_to(sums, sums_out.shape)
    sums_in[me] = jnp.broadcast_to(sums, sums_out.shape)
    for offset in offsets:
        send(SUMS, peer_of(offset))

    forward(seq_grad, spec_a, spec_b)
    put_product(
        spec_a[...] * spec_c[...] + spec_b[...] * spec_d[...],
        spec_b[...] * spec_c[...] - spec_a[...] * spec_d[...],
    )
    inverse(back_out, BACK)
    local[2].wait()

    def finish_conv(index, conv):
        out[:, cols(index)] = conv

    def finish_back(index, back):
        value_grad[:, cols(index)] = back

    finish_conv(me, conv_out[seq_rows(me), :])
    finish_back(me, back_out[seq_rows(me), :])
    for kind, finish, landed in ((CONV, finish_conv, conv_in), (BACK, finish_back, back_in)):
        for offset in reversed(offsets):
            peer = peer_of(offset)
            copy_of(kind, peer, peer).wait_recv()
            finish(peer, landed[peer])
    receive(SUMS)
    gain[...] = sums_in[owner[me]][:1, :]
    for kind in range(6):
        for offset in offsets:
            peer = peer_of(offset)
            copy_of(kind, peer, me).wait_send()


def finish_kernel(
    conv, back, value, gate, cot, skip, gathered, output, value_grad, gate_grad, gain
):
    gate_rows, cot_rows = gate[...].astype(jnp.float32), cot[...].astype(jnp.float32)
    grads = (cot_rows * gate_rows).astype(jnp.bfloat16).astype(jnp.float32)
    mixed = conv[...].astype(jnp.float32) + skip[...] * value[...].astype(jnp.float32)
    output[...] = (gate_rows * mixed).astype(jnp.bfloat16)
    gate_grad[...] = (cot_rows * mixed).astype(jnp.bfloat16)
    value_grad[...] = (back[...].astype(jnp.float32) + skip[...] * grads).astype(jnp.bfloat16)
    gain[...] = gathered[...]


def fused_body(value, gate, long_filter, skip_gain, cotangent, owner_map):
    n = lax.axis_size("seq")
    rows, group = value.shape
    chans = group // n
    length = rows * n
    base_cos, base_sin, turn = base_tables(length)
    anywhere = pl.BlockSpec(memory_space=pltpu.HBM)
    vmem = pl.BlockSpec(memory_space=pltpu.VMEM)
    bf16, f32 = jnp.bfloat16, jnp.float32
    table = pltpu.VMEM((length, length), bf16)
    spec = pltpu.VMEM((length, chans), f32)
    tokens = pltpu.VMEM((rows, group), bf16)
    sequence = pltpu.VMEM((length, chans), bf16)
    landing = pltpu.VMEM((n, rows, chans), bf16)
    conv, back, gain = pl.pallas_call(
        functools.partial(fused_kernel, n),
        out_shape=(
            jax.ShapeDtypeStruct((rows, group), bf16),
            jax.ShapeDtypeStruct((rows, group), bf16),
            jax.ShapeDtypeStruct((1, chans), f32),
        ),
        in_specs=[
            anywhere,
            anywhere,
            anywhere,
            anywhere,
            vmem,
            pl.BlockSpec(memory_space=pltpu.SMEM),
            anywhere,
            anywhere,
            anywhere,
        ],
        out_specs=(vmem, vmem, vmem),
        scratch_shapes=[
            pltpu.VMEM(base_cos.shape, f32),
            pltpu.VMEM(base_sin.shape, f32),
            pltpu.VMEM(turn.shape, f32),
            tokens,
            tokens,
            tokens,
            tokens,
            table,
            table,
            table,
            table,
            sequence,
            pltpu.VMEM((n, chans, rows), bf16),
            sequence,
            sequence,
            spec,
            spec,
            spec,
            spec,
            pltpu.VMEM((length, 2 * chans), bf16),
            pltpu.VMEM((length, 2 * chans), bf16),
            sequence,
            sequence,
            landing,
            landing,
            pltpu.VMEM((8, chans), f32),
            pltpu.VMEM((n, 8, chans), f32),
            pltpu.SemaphoreType.DMA((6, n)),
            pltpu.SemaphoreType.DMA((6, n)),
            pltpu.SemaphoreType.DMA((8,)),
        ],
        compiler_params=pltpu.CompilerParams(
            collective_id=0, has_side_effects=True
        ),
    )(
        value,
        long_filter,
        gate,
        cotangent,
        skip_gain.reshape(1, group),
        owner_map,
        base_cos,
        base_sin,
        turn,
    )
    output, value_grad, gate_grad, gain = pl.pallas_call(
        finish_kernel,
        grid=(2,),
        out_shape=(
            jax.ShapeDtypeStruct((rows, group), bf16),
            jax.ShapeDtypeStruct((rows, group), bf16),
            jax.ShapeDtypeStruct((rows, group), bf16),
            jax.ShapeDtypeStruct((1, chans), f32),
        ),
        in_specs=[pl.BlockSpec((rows // 2, group), lambda i: (i, 0))] * 5
        + [pl.BlockSpec((1, group), lambda i: (0, 0)), pl.BlockSpec((1, chans), lambda i: (0, 0))],
        out_specs=[pl.BlockSpec((rows // 2, group), lambda i: (i, 0))] * 3
        + [pl.BlockSpec((1, chans), lambda i: (0, 0))],
    )(conv, back, value, gate, cotangent, skip_gain.reshape(1, group), gain)
    return (output, value_grad, gate_grad, gain.reshape(1, 1, chans))


def body(value, gate, long_filter, skip_gain, cotangent, owner_map):
    n = lax.axis_size("seq")
    rows, group = value.shape
    aligned = rows % LANES == 0 and group % (n * LANES) == 0 and n % 2 == 0
    tables_fit = 8 * (rows * n) ** 2 <= 16 * 2**20
    chosen = fused_body if aligned and tables_fit else split_body
    return chosen(value, gate, long_filter, skip_gain, cotangent, owner_map)


def solution(mesh):
    in_specs = (
        P("seq", "chan"),
        P("seq", "chan"),
        P("chan", "seq"),
        P("chan"),
        P("seq", "chan"),
        P(),
    )
    out_specs = (P("seq", "chan"), P("seq", "chan"), P("seq", "chan"), P("chan", "seq", None))
    return jax.shard_map(body, mesh=mesh, in_specs=in_specs, out_specs=out_specs, check_vma=False)
```

```python
import functools
import math

import jax
import jax.numpy as jnp
import numpy as np
from jax import lax
from jax.experimental import pallas as pl
from jax.experimental.pallas import tpu as pltpu
from jax.sharding import PartitionSpec as P

HIGHEST = lax.Precision.HIGHEST


def dft_table(size):
    index = jnp.arange(size, dtype=jnp.int32)
    phase = index[:, None] * index[None, :] % size
    angle = 2.0 * math.pi / size * phase.astype(jnp.float32)
    return (jnp.cos(angle), jnp.sin(angle))


def make_tables(outer, inner):
    cos_outer, sin_outer = dft_table(outer)
    cos_inner, sin_inner = dft_table(inner)
    total = outer * inner
    phase = (
        jnp.arange(outer, dtype=jnp.int32)[:, None]
        * jnp.arange(inner, dtype=jnp.int32)[None, :]
        % total
    )
    angle = 2.0 * math.pi / total * phase.astype(jnp.float32)
    return (cos_outer, sin_outer, cos_inner, sin_inner, jnp.cos(angle), jnp.sin(angle))


def forward_dft(signal, tables):
    cos_outer, sin_outer, cos_inner, sin_inner, turn_cos, turn_sin = tables
    blocks = signal.shape[0]
    real_part = jnp.einsum("kn,ncb->ckb", cos_outer[:, :blocks], signal, precision=HIGHEST)
    imag_part = -jnp.einsum("kn,ncb->ckb", sin_outer[:, :blocks], signal, precision=HIGHEST)
    twisted_real = real_part * turn_cos + imag_part * turn_sin
    twisted_imag = imag_part * turn_cos - real_part * turn_sin
    spec_real = jnp.einsum("ckn,nm->ckm", twisted_real, cos_inner, precision=HIGHEST) + jnp.einsum(
        "ckn,nm->ckm", twisted_imag, sin_inner, precision=HIGHEST
    )
    spec_imag = jnp.einsum("ckn,nm->ckm", twisted_imag, cos_inner, precision=HIGHEST) - jnp.einsum(
        "ckn,nm->ckm", twisted_real, sin_inner, precision=HIGHEST
    )
    return (spec_real, spec_imag)


def inverse_dft(spec_real, spec_imag, tables, blocks):
    cos_outer, sin_outer, cos_inner, sin_inner, turn_cos, turn_sin = tables
    total = cos_outer.shape[0] * cos_inner.shape[0]
    inner_real = jnp.einsum("ckm,mn->ckn", spec_real, cos_inner, precision=HIGHEST) - jnp.einsum(
        "ckm,mn->ckn", spec_imag, sin_inner, precision=HIGHEST
    )
    inner_imag = jnp.einsum("ckm,mn->ckn", spec_real, sin_inner, precision=HIGHEST) + jnp.einsum(
        "ckm,mn->ckn", spec_imag, cos_inner, precision=HIGHEST
    )
    turned_real = inner_real * turn_cos - inner_imag * turn_sin
    turned_imag = inner_real * turn_sin + inner_imag * turn_cos
    result = jnp.einsum(
        "nk,ckb->ncb", cos_outer[:blocks, :], turned_real, precision=HIGHEST
    ) - jnp.einsum("nk,ckb->ncb", sin_outer[:blocks, :], turned_imag, precision=HIGHEST)
    return result / total


def causal_conv(sent_value, filter_spec, tables):
    value_real, value_imag = forward_dft(sent_value.astype(jnp.float32), tables)
    filter_real, filter_imag = filter_spec
    product_real = value_real * filter_real - value_imag * filter_imag
    product_imag = value_real * filter_imag + value_imag * filter_real
    return inverse_dft(product_real, product_imag, tables, sent_value.shape[0]).astype(jnp.bfloat16)


def transposed_conv(sent_grad, filter_spec, tables):
    grad_real, grad_imag = forward_dft(sent_grad.astype(jnp.float32), tables)
    filter_real, filter_imag = filter_spec
    product_real = grad_real * filter_real + grad_imag * filter_imag
    product_imag = grad_imag * filter_real - grad_real * filter_imag
    return inverse_dft(product_real, product_imag, tables, sent_grad.shape[0]).astype(jnp.bfloat16)


def split_body(value, gate, long_filter, skip_gain, cotangent, owner_map):
    blocks = lax.axis_size("seq")
    tok_rows = value.shape[0]
    group = value.shape[1]
    per_device = group // blocks
    value_rows = value.astype(jnp.float32)
    gate_rows = gate.astype(jnp.float32)
    grad_rows = (cotangent.astype(jnp.float32) * gate_rows).astype(jnp.bfloat16)
    value_major = value.T
    grad_major = grad_rows.T
    tables = make_tables(2 * blocks, tok_rows)
    value_split = value_major.reshape(blocks, per_device, tok_rows)
    filter_split = long_filter.reshape(blocks, per_device, tok_rows)
    grad_split = grad_major.reshape(blocks, per_device, tok_rows)
    sent_value, sent_filter = (
        lax.all_to_all(value_split, "seq", split_axis=0, concat_axis=0, tiled=True),
        lax.all_to_all(filter_split, "seq", split_axis=0, concat_axis=0, tiled=True),
    )
    filter_spec = forward_dft(sent_filter.astype(jnp.float32), tables)
    conv_back = lax.all_to_all(
        causal_conv(sent_value, filter_spec, tables), "seq", split_axis=0, concat_axis=0, tiled=True
    )
    sent_grad = lax.all_to_all(grad_split, "seq", split_axis=0, concat_axis=0, tiled=True)
    grad_back = lax.all_to_all(
        transposed_conv(sent_grad, filter_spec, tables),
        "seq",
        split_axis=0,
        concat_axis=0,
        tiled=True,
    )
    conv_rows = conv_back.reshape(group, tok_rows).T.astype(jnp.float32)
    mixed = conv_rows + skip_gain * value_rows
    output = (gate_rows * mixed).astype(jnp.bfloat16)
    gate_grad = (cotangent.astype(jnp.float32) * mixed).astype(jnp.bfloat16)
    back_rows = grad_back.reshape(group, tok_rows).T.astype(jnp.float32)
    grad_float = grad_rows.astype(jnp.float32)
    value_grad = (back_rows + skip_gain * grad_float).astype(jnp.bfloat16)
    scale = 1.0 / math.sqrt(tok_rows * blocks)
    local_sums = (
        jnp.sum(sent_value.astype(jnp.float32) * sent_grad.astype(jnp.float32), axis=(0, 2)) * scale
    )
    gathered = lax.all_gather(local_sums.reshape(1, per_device), "seq", axis=0, tiled=True)
    mine = owner_map[lax.axis_index("seq")]
    summed = lax.dynamic_slice_in_dim(gathered, mine, 1, 0)
    gain_grad = summed.reshape(1, 1, per_device)
    return (output, value_grad, gate_grad, gain_grad)


LANES = 128
FILTER, VALUE, GRAD, CONV, BACK, SUMS = range(6)
MESH = pl.DeviceIdType.MESH


def base_tables(length):
    unit = 2.0 * math.pi / (16 * length)
    row = 4 * np.arange(length, dtype=np.int64)[:, None] + 1
    lane = 4 * np.arange(LANES, dtype=np.int64)[None, :] + 1
    angle = unit * (row * lane % (16 * length))
    block = 4 * LANES * np.arange(length // LANES, dtype=np.int64)[None, :]
    step = unit * (row * block % (16 * length))
    quarter = unit * row
    turn = np.concatenate([np.cos(step), np.sin(step), np.cos(quarter), np.sin(quarter)], axis=1)
    turn = np.pad(turn, ((0, 0), (0, -turn.shape[1] % LANES)))
    return tuple(t.astype(np.float32) for t in (np.cos(angle), np.sin(angle), turn))


def split(wide):
    high = wide.astype(jnp.bfloat16)
    return high, (wide - high.astype(jnp.float32)).astype(jnp.bfloat16)


def fused_kernel(
    n,
    value,
    filt,
    gate,
    cot,
    skip,
    owner,
    base_cos_any,
    base_sin_any,
    turn_any,
    out,
    value_grad,
    gain,
    base_cos,
    base_sin,
    turn,
    value_loc,
    gate_loc,
    cot_loc,
    grad_loc,
    cos_hi,
    cos_lo,
    sin_hi,
    sin_lo,
    seq_value,
    seq_filter,
    taps,
    seq_grad,
    spec_c,
    spec_d,
    spec_a,
    spec_b,
    prod_cos,
    prod_sin,
    conv_out,
    back_out,
    conv_in,
    back_in,
    sums_out,
    sums_in,
    send_sem,
    recv_sem,
    local_sem,
):
    me = lax.axis_index("seq")
    rows, group = value.shape
    chans = group // n
    length = rows * n
    half = length // 2
    offsets = sorted(range(1, n), key=lambda i: abs(2 * i - n))
    blocks = length // LANES

    def peer_of(offset):
        return lax.rem(me + offset, n)

    def cols(index):
        return pl.ds(pl.multiple_of(index * chans, chans), chans)

    def seq_rows(index):
        return pl.ds(pl.multiple_of(index * rows, rows), rows)

    def transfer(kind, source, target, peer, sender):
        return pltpu.make_async_remote_copy(
            src_ref=source,
            dst_ref=target,
            send_sem=send_sem.at[kind, peer],
            recv_sem=recv_sem.at[kind, sender],
            device_id={"seq": peer},
            device_id_type=MESH,
        )

    def copy_of(kind, peer, sender):
        if kind == FILTER:
            pair = filt.at[cols(peer), :], seq_filter.at[sender]
        elif kind == VALUE:
            pair = value.at[:, cols(peer)], seq_value.at[seq_rows(sender), :]
        elif kind == GRAD:
            pair = grad_loc.at[:, cols(peer)], seq_grad.at[seq_rows(sender), :]
        elif kind == CONV:
            pair = conv_out.at[seq_rows(peer), :], conv_in.at[sender]
        elif kind == BACK:
            pair = back_out.at[seq_rows(peer), :], back_in.at[sender]
        else:
            pair = sums_out, sums_in.at[sender]
        return transfer(kind, *pair, peer, sender)

    def send(kind, peer):
        copy_of(kind, peer, me).start()

    def receive(kind):
        for offset in reversed(offsets):
            peer = peer_of(offset)
            copy_of(kind, peer, peer).wait_recv()

    barrier = pltpu.get_barrier_semaphore()
    for offset in offsets:
        pl.semaphore_signal(barrier, inc=1, device_id={"seq": peer_of(offset)}, device_id_type=MESH)
    local = [
        pltpu.make_async_copy(gate, gate_loc, local_sem.at[0]),
        pltpu.make_async_copy(cot, cot_loc, local_sem.at[1]),
        pltpu.make_async_copy(value, value_loc, local_sem.at[2]),
        pltpu.make_async_copy(filt.at[cols(me), :], seq_filter.at[me], local_sem.at[3]),
        pltpu.make_async_copy(value.at[:, cols(me)], seq_value.at[seq_rows(me), :], local_sem.at[4]),
        pltpu.make_async_copy(base_cos_any, base_cos, local_sem.at[5]),
        pltpu.make_async_copy(base_sin_any, base_sin, local_sem.at[6]),
        pltpu.make_async_copy(turn_any, turn, local_sem.at[7]),
    ]
    for copy in local:
        copy.start()
    pl.semaphore_wait(barrier, n - 1)
    for kind in (FILTER, VALUE):
        for offset in offsets:
            send(kind, peer_of(offset))

    local[0].wait()
    local[1].wait()
    grad_loc[...] = (cot_loc[...].astype(jnp.float32) * gate_loc[...].astype(jnp.float32)).astype(
        jnp.bfloat16
    )
    seq_grad[seq_rows(me), :] = grad_loc[:, cols(me)]
    for offset in offsets:
        send(GRAD, peer_of(offset))

    for copy in local[5:]:
        copy.wait()

    @pl.loop(0, length // LANES)
    def _(step):
        at = pl.ds(pl.multiple_of(step * LANES, LANES), LANES)
        lane_cos, lane_sin = base_cos[at, :], base_sin[at, :]
        for block in range(blocks):
            block_cos = turn[at, block : block + 1]
            block_sin = turn[at, blocks + block : blocks + block + 1]
            to = pl.ds(block * LANES, LANES)
            cos_hi[at, to], cos_lo[at, to] = split(lane_cos * block_cos - lane_sin * block_sin)
            sin_hi[at, to], sin_lo[at, to] = split(lane_sin * block_cos + lane_cos * block_sin)

    def forward(signal, real, imag):
        for high, low, spec in ((cos_hi, cos_lo, real), (sin_hi, sin_lo, imag)):
            spec[...] = jnp.dot(
                high[...], signal[...], preferred_element_type=jnp.float32
            ) + jnp.dot(low[...], signal[...], preferred_element_type=jnp.float32)

    def put_product(on_cos, on_sin):
        for wide, store in ((on_cos, prod_cos), (on_sin, prod_sin)):
            high, low = split(wide)
            store[:, :chans] = high
            store[:, chans:] = low

    def inverse(result, kind):
        mine = me // (n // 2)

        @pl.loop(0, 2)
        def _(step):
            part = lax.rem(mine + 1 + step, 2)
            at = pl.ds(pl.multiple_of(part * half, half), half)
            both = jnp.dot(
                cos_hi[at, :], prod_cos[...], preferred_element_type=jnp.float32
            ) + jnp.dot(sin_hi[at, :], prod_sin[...], preferred_element_type=jnp.float32)
            low = jnp.dot(
                cos_lo[at, :], prod_cos[:, :chans], preferred_element_type=jnp.float32
            ) + jnp.dot(sin_lo[at, :], prod_sin[:, :chans], preferred_element_type=jnp.float32)
            result[at, :] = (both[:, :chans] + (both[:, chans:] + low)).astype(jnp.bfloat16)
            for index in range(n // 2):
                to = part * (n // 2) + lax.rem(me + index, n // 2)

                @pl.when(to != me)
                def _():
                    send(kind, to)

    local[3].wait()
    receive(FILTER)
    for index in range(n):
        taps[index * rows : (index + 1) * rows, :] = (
            seq_filter[index].astype(jnp.float32).T.astype(jnp.bfloat16)
        )
    forward(taps, spec_a, spec_b)
    quarter_cos = turn[:, 2 * blocks : 2 * blocks + 1] * (1.0 / length)
    quarter_sin = turn[:, 2 * blocks + 1 : 2 * blocks + 2] * (1.0 / length)
    spec_c[...] = spec_a[...] * quarter_cos + spec_b[...] * quarter_sin
    spec_d[...] = spec_b[...] * quarter_cos - spec_a[...] * quarter_sin

    local[4].wait()
    receive(VALUE)
    forward(seq_value, spec_a, spec_b)
    put_product(
        spec_a[...] * spec_c[...] - spec_b[...] * spec_d[...],
        spec_a[...] * spec_d[...] + spec_b[...] * spec_c[...],
    )
    inverse(conv_out, CONV)

    receive(GRAD)
    sums = jnp.sum(
        seq_value[...].astype(jnp.float32) * seq_grad[...].astype(jnp.float32), axis=0, keepdims=True
    ) * (1.0 / math.sqrt(length))
    sums_out[...] = jnp.broadcast_to(sums, sums_out.shape)
    sums_in[me] = jnp.broadcast_to(sums, sums_out.shape)
    for offset in offsets:
        send(SUMS, peer_of(offset))

    forward(seq_grad, spec_a, spec_b)
    put_product(
        spec_a[...] * spec_c[...] + spec_b[...] * spec_d[...],
        spec_b[...] * spec_c[...] - spec_a[...] * spec_d[...],
    )
    inverse(back_out, BACK)
    local[2].wait()

    def finish_conv(index, conv):
        out[:, cols(index)] = conv

    def finish_back(index, back):
        value_grad[:, cols(index)] = back

    finish_conv(me, conv_out[seq_rows(me), :])
    finish_back(me, back_out[seq_rows(me), :])
    for kind, finish, landed in ((CONV, finish_conv, conv_in), (BACK, finish_back, back_in)):
        for offset in reversed(offsets):
            peer = peer_of(offset)
            copy_of(kind, peer, peer).wait_recv()
            finish(peer, landed[peer])
    receive(SUMS)
    gain[...] = sums_in[owner[me]][:1, :]
    for kind in range(6):
        for offset in offsets:
            peer = peer_of(offset)
            copy_of(kind, peer, me).wait_send()


def finish_kernel(
    conv, back, value, gate, cot, skip, gathered, output, value_grad, gate_grad, gain
):
    gate_rows, cot_rows = gate[...].astype(jnp.float32), cot[...].astype(jnp.float32)
    grads = (cot_rows * gate_rows).astype(jnp.bfloat16).astype(jnp.float32)
    mixed = conv[...].astype(jnp.float32) + skip[...] * value[...].astype(jnp.float32)
    output[...] = (gate_rows * mixed).astype(jnp.bfloat16)
    gate_grad[...] = (cot_rows * mixed).astype(jnp.bfloat16)
    value_grad[...] = (back[...].astype(jnp.float32) + skip[...] * grads).astype(jnp.bfloat16)
    gain[...] = gathered[...]


def fused_body(value, gate, long_filter, skip_gain, cotangent, owner_map):
    n = lax.axis_size("seq")
    rows, group = value.shape
    chans = group // n
    length = rows * n
    base_cos, base_sin, turn = base_tables(length)
    anywhere = pl.BlockSpec(memory_space=pltpu.HBM)
    vmem = pl.BlockSpec(memory_space=pltpu.VMEM)
    bf16, f32 = jnp.bfloat16, jnp.float32
    table = pltpu.VMEM((length, length), bf16)
    spec = pltpu.VMEM((length, chans), f32)
    tokens = pltpu.VMEM((rows, group), bf16)
    sequence = pltpu.VMEM((length, chans), bf16)
    landing = pltpu.VMEM((n, rows, chans), bf16)
    conv, back, gain = pl.pallas_call(
        functools.partial(fused_kernel, n),
        out_shape=(
            jax.ShapeDtypeStruct((rows, group), bf16),
            jax.ShapeDtypeStruct((rows, group), bf16),
            jax.ShapeDtypeStruct((1, chans), f32),
        ),
        in_specs=[
            anywhere,
            anywhere,
            anywhere,
            anywhere,
            vmem,
            pl.BlockSpec(memory_space=pltpu.SMEM),
            anywhere,
            anywhere,
            anywhere,
        ],
        out_specs=(vmem, vmem, vmem),
        scratch_shapes=[
            pltpu.VMEM(base_cos.shape, f32),
            pltpu.VMEM(base_sin.shape, f32),
            pltpu.VMEM(turn.shape, f32),
            tokens,
            tokens,
            tokens,
            tokens,
            table,
            table,
            table,
            table,
            sequence,
            pltpu.VMEM((n, chans, rows), bf16),
            sequence,
            sequence,
            spec,
            spec,
            spec,
            spec,
            pltpu.VMEM((length, 2 * chans), bf16),
            pltpu.VMEM((length, 2 * chans), bf16),
            sequence,
            sequence,
            landing,
            landing,
            pltpu.VMEM((8, chans), f32),
            pltpu.VMEM((n, 8, chans), f32),
            pltpu.SemaphoreType.DMA((6, n)),
            pltpu.SemaphoreType.DMA((6, n)),
            pltpu.SemaphoreType.DMA((8,)),
        ],
        compiler_params=pltpu.CompilerParams(
            collective_id=0, has_side_effects=True
        ),
    )(
        value,
        long_filter,
        gate,
        cotangent,
        skip_gain.reshape(1, group),
        owner_map,
        base_cos,
        base_sin,
        turn,
    )
    output, value_grad, gate_grad, gain = pl.pallas_call(
        finish_kernel,
        grid=(2,),
        out_shape=(
            jax.ShapeDtypeStruct((rows, group), bf16),
            jax.ShapeDtypeStruct((rows, group), bf16),
            jax.ShapeDtypeStruct((rows, group), bf16),
            jax.ShapeDtypeStruct((1, chans), f32),
        ),
        in_specs=[pl.BlockSpec((rows // 2, group), lambda i: (i, 0))] * 5
        + [pl.BlockSpec((1, group), lambda i: (0, 0)), pl.BlockSpec((1, chans), lambda i: (0, 0))],
        out_specs=[pl.BlockSpec((rows // 2, group), lambda i: (i, 0))] * 3
        + [pl.BlockSpec((1, chans), lambda i: (0, 0))],
    )(conv, back, value, gate, cotangent, skip_gain.reshape(1, group), gain)
    return (output, value_grad, gate_grad, gain.reshape(1, 1, chans))


def body(value, gate, long_filter, skip_gain, cotangent, owner_map):
    n = lax.axis_size("seq")
    rows, group = value.shape
    aligned = rows % LANES == 0 and group % (n * LANES) == 0 and n % 2 == 0
    tables_fit = 8 * (rows * n) ** 2 <= 16 * 2**20
    chosen = fused_body if aligned and tables_fit else split_body
    return chosen(value, gate, long_filter, skip_gain, cotangent, owner_map)


def solution(mesh):
    in_specs = (
        P("seq", "chan"),
        P("seq", "chan"),
        P("chan", "seq"),
        P("chan"),
        P("seq", "chan"),
        P(),
    )
    out_specs = (P("seq", "chan"), P("seq", "chan"), P("seq", "chan"), P("chan", "seq", None))
    return jax.shard_map(body, mesh=mesh, in_specs=in_specs, out_specs=out_specs, check_vma=False)
```
